32 devices in a mesh: dp: 16 (over z, y, core), tensor: 2 (over x).
Axes of the slice: x: 2, y: 2, z: 4, core: 2. Of those that a mesh axis runs over, the one named last changes fastest.
Arguments:
- layer_input: bfloat16 [12288, 1024], P(('dp', 'tensor')), may hold values from -6 to 6
- norm_gain: bfloat16 [1024], P('dp'), may hold values from 0.5 to 1.5
- gate_proj: bfloat16 [1024, 2048], P('dp', 'tensor'), may hold values from -0.1875 to 0.1875
- value_proj: bfloat16 [1024, 2048], P('dp', 'tensor'), may hold values from -0.1875 to 0.1875
- bc_proj: bfloat16 [1024, 256], P('dp'), may hold values from -0.1875 to 0.1875
- step_proj: bfloat16 [1024, 32], P('dp', 'tensor'), may hold values from -0.1875 to 0.1875
- out_proj: bfloat16 [2048, 1024], P('tensor', 'dp'), may hold values from -0.125 to 0.125
- value_taps: float32 [4, 2048], P(None, 'tensor'), may hold values from -0.5 to 0.5
- value_bias: float32 [2048], P('tensor'), may hold values from -0.5 to 0.5
- bc_taps: float32 [4, 256], replicated, may hold values from -0.5 to 0.5
- bc_bias: float32 [256], replicated, may hold values from -0.5 to 0.5
- step_shift: float32 [32], P('tensor'), may hold values from -6 to -2
- log_rate: float32 [32], P('tensor'), may hold values from 0 to 2.77
- skip_gain: float32 [32], P('tensor'), may hold values from 0.5 to 1.5
- gate_gain: float32 [2048], P('tensor'), may hold values from 0.5 to 1.5
- cotangent: bfloat16 [12288, 1024], P(('dp', 'tensor')), may hold values from -6 to 6
Outputs:
- layer_output: bfloat16 [12288, 1024], P(('dp', 'tensor'))
- input_grad: float32 [12288, 1024], P(('dp', 'tensor'))
- gain_grad: float32 [1024], P('dp')
- gate_grad: float32 [1024, 2048], P('dp', 'tensor')
- value_grad: float32 [1024, 2048], P('dp', 'tensor')
- bc_grad: float32 [1024, 256], P('dp')
- step_grad: float32 [1024, 32], P('dp', 'tensor')
- out_grad: float32 [2048, 1024], P('tensor', 'dp')
- taps_grad: float32 [4, 2048], P(None, 'tensor')
- bias_grad: float32 [2048], P('tensor')
- bctaps_grad: float32 [4, 256], replicated
- bcbias_grad: float32 [256], replicated
- shift_grad: float32 [32], P('tensor')
- rate_grad: float32 [32], P('tensor')
- skip_grad: float32 [32], P('tensor')
- gating_grad: float32 [2048], P('tensor')
The draws below stay inside these ranges and needn't reach their ends.
All inputs are finite; a program needn't handle non-finite values.
Results may differ from the reference program's by a relative error of at most 0.0089.
Values may be sent and summed in bfloat16 or wider, within the bound.
No kernel may reach another device: no remote copies, remote signals or barrier semaphores. Data moves between devices by JAX's collectives and lax.ppermute only.
A program may use at most 192 MiB of HBM per device.

```python
import jax
import jax.numpy as jnp
from jax import lax

D = 1024
H = 32
N = 128
K = 4
SEQ_LEN = 768
E = 2048
TOKENS = 12288
N_DP = 16


def spiked(result, key, source, target, parts, factor):
    def block_of(axis_at):
        return (jnp.arange(result.shape[axis_at]) // (result.shape[axis_at] // parts)).reshape((-1,) + (1,) * (result.ndim - 1 - axis_at))

    one_side = jax.random.permutation(key, parts)[block_of(target)]
    far = (block_of(target) + parts // 2) % parts
    return jnp.where((block_of(source) == one_side) | (block_of(source) == far), factor * result, result)


def steps_of(key, shape, pieces, least, largest):
    def one(dim, blocks):
        draws = jax.random.uniform(jax.random.fold_in(jax.random.fold_in(key, 6), dim), (blocks,), jnp.float32, least / len(pieces), largest / len(pieces))
        return jnp.repeat(jnp.exp(draws), shape[dim] // blocks).reshape((-1,) + (1,) * (len(shape) - dim - 1))

    level = one(*pieces[0])
    for cut in pieces[1:]:
        level = level * one(*cut)
    return level


def centred(own_key, shape, scale, most, cuts=(), dtype=jnp.bfloat16):
    values = jax.random.normal(own_key, shape, jnp.float32) * scale
    if len(cuts) > 0:
        values = steps_of(own_key, shape, cuts, -0.22, 0.18) * values
    return jnp.clip(values, min=-most, max=most).astype(dtype)


def gaussian_with(rng, shape, spread, limit, pieces, heavy, held_as=jnp.bfloat16):
    drawn = spread * jax.random.normal(rng, shape, jnp.float32)
    if pieces:
        drawn = drawn * steps_of(rng, shape, pieces, -0.22, 0.18)
    return jnp.clip(spiked(drawn, jax.random.fold_in(rng, 3), *heavy), -limit, limit).astype(held_as)


def setup_inputs(seed: int = 0) -> dict:
    key_of = jax.random.split(jax.random.key(seed), 17)
    layer_input = gaussian_with(key_of[0], (TOKENS, D), 1.0, 6.0, ((0, 32),), (0, 1, 32, 2.75))
    norm_gain = jnp.clip(1.0 + 0.1 * jax.random.normal(key_of[1], (D,), jnp.float32), 0.5, 1.5).astype(jnp.bfloat16)
    gate_proj = centred(key_of[2], (D, E), D ** -0.5, 0.1875, ((0, 16), (1, 2)))
    value_proj = centred(key_of[3], (D, E), D ** -0.5, 0.1875, ((0, 16), (1, 2)))
    bc_proj = centred(key_of[4], (D, 2 * N), D ** -0.5, 0.1875, ((0, 16),))
    step_proj = centred(key_of[5], (D, H), D ** -0.5, 0.1875, ((0, 16), (1, 2)))
    out_proj = centred(key_of[6], (E, D), E ** -0.5, 0.125, ((0, 2), (1, 16)))
    value_taps = jnp.clip(jax.random.uniform(key_of[7], (K, E), jnp.float32, -0.5, 0.5) * steps_of(key_of[7], (K, E), ((1, 2),), -0.4, 0.0), -0.5, 0.5)
    value_bias = jnp.clip(jax.random.uniform(key_of[8], (E,), jnp.float32, -0.5, 0.5) * steps_of(key_of[8], (E,), ((0, 2),), -0.4, 0.0), -0.5, 0.5)
    bc_taps = jnp.clip(jax.random.uniform(key_of[9], (K, 2 * N), jnp.float32, -0.5, 0.5), -0.5, 0.5)
    bc_bias = jnp.clip(jax.random.uniform(key_of[10], (2 * N,), jnp.float32, -0.5, 0.5), -0.5, 0.5)
    step_shift = jnp.clip(-6.0 + 4.0 * jax.random.uniform(key_of[11], (H,), jnp.float32) ** steps_of(key_of[11], (H,), ((0, 2),), -0.2, 0.2), -6.0, -2.0)
    log_rate = jnp.clip(2.77 * jax.random.uniform(key_of[12], (H,), jnp.float32) ** steps_of(key_of[12], (H,), ((0, 2),), -0.2, 0.2), 0.0, 2.77)
    skip_gain = jnp.clip(0.5 + 1.0 * jax.random.uniform(key_of[13], (H,), jnp.float32) ** steps_of(key_of[13], (H,), ((0, 2),), -0.2, 0.2), 0.5, 1.5)
    gate_gain = jnp.clip(1.0 + 0.1 * jax.random.normal(key_of[14], (E,), jnp.float32), 0.5, 1.5)
    cotangent = gaussian_with(key_of[15], (TOKENS, D), 1.0, 6.0, ((0, 32),), (0, 1, 32, 2.75))
    return {"layer_input": layer_input, "norm_gain": norm_gain, "gate_proj": gate_proj, "value_proj": value_proj, "bc_proj": bc_proj, "step_proj": step_proj, "out_proj": out_proj, "value_taps": value_taps, "value_bias": value_bias, "bc_taps": bc_taps, "bc_bias": bc_bias, "step_shift": step_shift, "log_rate": log_rate, "skip_gain": skip_gain, "gate_gain": gate_gain, "cotangent": cotangent}


EPS = 1e-05
FULL_PRECISION = lax.Precision.HIGHEST

def rms_scale(rows, gain):
    inverse = lax.rsqrt(lax.optimization_barrier(jnp.mean(rows * rows, axis=-1, keepdims=True)) + EPS)
    return rows * inverse * gain[None, :]

def causal_conv(signal, taps, offset):
    width = taps.shape[0]
    length = signal.shape[0]
    padded = jnp.pad(signal, ((width - 1, 0), (0, 0)))
    total = jnp.zeros(signal.shape, jnp.float32) + offset[None, :]
    for position in range(width):
        total = total + taps[position][None, :] * padded[position:position + length]
    return total

def bc_act(bc_pre, bc_taps, bc_bias):
    return jax.nn.silu(causal_conv(bc_pre, bc_taps, bc_bias))

def mixer_ref(value_pre, shared, step_pre, value_taps, value_bias, step_shift, log_rate, skip_gain):
    head_count = step_pre.shape[1]
    length = value_pre.shape[0]
    state_dim = shared.shape[1] // 2
    head_dim = value_pre.shape[1] // head_count
    values = jax.nn.silu(causal_conv(value_pre, value_taps, value_bias))
    b_in = shared[:, :state_dim]
    c_out = shared[:, state_dim:]
    timestep = jax.nn.softplus(step_pre + step_shift[None, :])
    log_decay = -jnp.exp(log_rate)[None, :] * timestep
    cumulative = jnp.cumsum(log_decay, axis=0)
    products = jnp.dot(c_out, b_in.T, precision=FULL_PRECISION)
    lower = jnp.arange(length)[:, None] >= jnp.arange(length)[None, :]
    head_values = values.reshape(length, head_count, head_dim).transpose(1, 0, 2)

    def one_head(scanned):
        cum_head, step_head, value_head = scanned
        exponent = jnp.where(lower, cum_head[:, None] - cum_head[None, :], -jnp.inf)
        mixing = products * jnp.exp(exponent) * step_head[None, :]
        return jnp.dot(mixing, value_head, precision=FULL_PRECISION)
    outputs = lax.map(one_head, (cumulative.T, timestep.T, head_values))
    combined = outputs.transpose(1, 0, 2).reshape(length, head_count * head_dim)
    return combined + values * jnp.repeat(skip_gain, head_dim)[None, :]

def reference(layer_input, norm_gain, gate_proj, value_proj, bc_proj, step_proj, out_proj, value_taps, value_bias, bc_taps, bc_bias, step_shift, log_rate, skip_gain, gate_gain, cotangent):
    sequences = layer_input.reshape(N_DP, SEQ_LEN, D)
    cot_seqs = cotangent.reshape(N_DP, SEQ_LEN, D)
    gain_f32 = norm_gain.astype(jnp.float32)

    def one_sequence(totals, scanned):
        rows, cot_rows = scanned
        rows_f32 = rows.astype(jnp.float32)
        normed, norm_back = jax.vjp(rms_scale, rows_f32, gain_f32)
        normed_b = normed.astype(jnp.bfloat16)
        gate_pre = jnp.dot(normed_b, gate_proj, preferred_element_type=jnp.float32)
        value_pre = jnp.dot(normed_b, value_proj, preferred_element_type=jnp.float32)
        bc_pre = jnp.dot(normed_b, bc_proj, preferred_element_type=jnp.float32)
        step_pre = jnp.dot(normed_b, step_proj, preferred_element_type=jnp.float32)
        shared, bc_back = jax.vjp(bc_act, bc_pre, bc_taps, bc_bias)
        mixed, mix_back = jax.vjp(mixer_ref, value_pre, shared, step_pre, value_taps, value_bias, step_shift, log_rate, skip_gain)
        gate_act = jax.nn.silu(gate_pre)
        gated = mixed * gate_act
        inv_rms = lax.rsqrt(lax.optimization_barrier(jnp.mean(gated * gated, axis=1, keepdims=True)) + EPS)
        gated_norm = (gated * inv_rms * gate_gain[None, :]).astype(jnp.bfloat16)
        output = (jnp.dot(gated_norm, out_proj, preferred_element_type=jnp.float32) + rows_f32).astype(jnp.bfloat16)
        out_part = jnp.dot(gated_norm.T, cot_rows, preferred_element_type=jnp.float32)
        normed_out = jnp.dot(cot_rows, out_proj.T, preferred_element_type=jnp.float32)
        scaled = normed_out * gate_gain[None, :]
        gating_part = lax.optimization_barrier(jnp.sum(normed_out * gated * inv_rms, axis=0))
        gated_grad = inv_rms * scaled - gated * inv_rms * inv_rms * inv_rms * lax.optimization_barrier(jnp.mean(scaled * gated, axis=1, keepdims=True))
        sigmoid = jax.nn.sigmoid(gate_pre)
        mixed_grad = gated_grad * gate_act
        gate_pre_grad = gated_grad * mixed * sigmoid * (1.0 + gate_pre * (1.0 - sigmoid))
        value_pre_grad, shared_grad, step_pre_grad, taps_part, bias_part, shift_part, rate_part, skip_part = mix_back(mixed_grad)
        bc_pre_grad, bctaps_part, bcbias_part = bc_back(shared_grad)
        gate_round = gate_pre_grad.astype(jnp.bfloat16)
        value_round = value_pre_grad.astype(jnp.bfloat16)
        step_round = step_pre_grad.astype(jnp.bfloat16)
        bc_round = bc_pre_grad.astype(jnp.bfloat16)
        normed_grad = jnp.dot(gate_round, gate_proj.T, preferred_element_type=jnp.float32)
        normed_grad = normed_grad + jnp.dot(value_round, value_proj.T, preferred_element_type=jnp.float32)
        normed_grad = normed_grad + jnp.dot(step_round, step_proj.T, preferred_element_type=jnp.float32)
        normed_grad = normed_grad + jnp.dot(bc_round, bc_proj.T, preferred_element_type=jnp.float32)
        rows_grad, gain_part = norm_back(normed_grad)
        input_grad = rows_grad + cot_rows.astype(jnp.float32)
        terms = (gain_part, jnp.dot(normed_b.T, gate_round, preferred_element_type=jnp.float32), jnp.dot(normed_b.T, value_round, preferred_element_type=jnp.float32), jnp.dot(normed_b.T, bc_round, preferred_element_type=jnp.float32), jnp.dot(normed_b.T, step_round, preferred_element_type=jnp.float32), out_part, taps_part, bias_part, bctaps_part, bcbias_part, shift_part, rate_part, skip_part, gating_part)
        return (jax.tree.map(jnp.add, totals, terms), (output, input_grad))
    initial = (jnp.zeros(norm_gain.shape, jnp.float32), jnp.zeros(gate_proj.shape, jnp.float32), jnp.zeros(value_proj.shape, jnp.float32), jnp.zeros(bc_proj.shape, jnp.float32), jnp.zeros(step_proj.shape, jnp.float32), jnp.zeros(out_proj.shape, jnp.float32), jnp.zeros(value_taps.shape, jnp.float32), jnp.zeros(value_bias.shape, jnp.float32), jnp.zeros(bc_taps.shape, jnp.float32), jnp.zeros(bc_bias.shape, jnp.float32), jnp.zeros(step_shift.shape, jnp.float32), jnp.zeros(log_rate.shape, jnp.float32), jnp.zeros(skip_gain.shape, jnp.float32), jnp.zeros(gate_gain.shape, jnp.float32))
    totals, results = lax.scan(one_sequence, initial, (sequences, cot_seqs))
    layer_output = results[0].reshape(TOKENS, D)
    input_grad = results[1].reshape(TOKENS, D)
    return (layer_output, input_grad, totals[0], totals[1], totals[2], totals[3], totals[4], totals[5], totals[6], totals[7], totals[8], totals[9], totals[10], totals[11], totals[12], totals[13])
```

```python
import functools

import jax
import jax.numpy as jnp
from jax import lax
from jax.experimental import pallas as pl
from jax.experimental.pallas import tpu as pltpu
from jax.sharding import PartitionSpec as P

EPS = 1e-05
LANES = 128
F32 = jnp.float32
BF16 = jnp.bfloat16
EXACT = lax.Precision.HIGHEST


def dot_mid(left, right, out=F32):
    return lax.dot_general(
        left, right, (((1,), (0,)), ((), ())), preferred_element_type=F32
    ).astype(out)


def dot_last(left, right, out=F32):
    return lax.dot_general(
        left, right, (((1,), (1,)), ((), ())), preferred_element_type=F32
    ).astype(out)


def dot_first(left, right, out=F32):
    return lax.dot_general(
        left, right, (((0,), (0,)), ((), ())), preferred_element_type=F32
    ).astype(out)


class Ring:
    def __init__(self, size):
        self.size = size
        self.chips = size // 2
        self.far = self.chips // 2
        self.order = list(range(0, self.chips, 2)) + [
            chip for chip in range(self.chips - 1, 0, -1) if chip % 2 == 1
        ]
        step = {
            chip: self.order[(at + 1) % self.chips] for at, chip in enumerate(self.order)
        }
        self.forth = [(c * 2 + k, step[c] * 2 + k) for c in range(self.chips) for k in (0, 1)]
        self.back = [(there, here) for here, there in self.forth]
        self.pair = [(at, at ^ 1) for at in range(size)]

    def sources(self):
        table = []
        for device in range(self.size):
            chip, core = device // 2, device % 2
            at = self.order.index(chip)
            table.append(
                [
                    self.order[(at + step) % self.chips] * 2 + (core ^ other)
                    for other in (0, 1)
                    for step in range(self.chips)
                ]
            )
        return jnp.asarray(table, jnp.int32)[lax.axis_index("dp")]

    def gather(self, shard, sources):
        rows = shard.shape[0]
        half = rows // 2
        pieces = {0: shard}
        up = down = shard
        for step in range(1, self.far):
            up = lax.ppermute(up, "dp", self.forth)
            down = lax.ppermute(down, "dp", self.back)
            pieces[self.chips - step], pieces[step] = up, down
        low = lax.ppermute(up[:half], "dp", self.forth)
        high = lax.ppermute(down[half:], "dp", self.back)
        parts = []
        for step in range(self.chips):
            parts += [low, high] if step == self.far else [pieces[step]]
        mine = stack_rows(parts)
        return place_rows(mine, lax.ppermute(mine, "dp", self.pair), sources, self.size)

    def scatter_sum(self, mine, other):
        total = mine + lax.ppermute(other, "dp", self.pair).astype(F32)
        rows = mine.shape[0] // self.chips
        half = rows // 2

        def piece(step):
            start = (step % self.chips) * rows
            return total[start : start + rows]

        up, down = piece(self.far)[:half], piece(self.far)[half:]
        for step in range(self.far - 1, -1, -1):
            up = lax.ppermute(up.astype(BF16), "dp", self.forth).astype(F32)
            down = lax.ppermute(down.astype(BF16), "dp", self.back).astype(F32)
            if step == self.far - 1:
                up = jnp.pad(up, ((0, half), (0, 0)))
                down = jnp.pad(down, ((half, 0), (0, 0)))
            if step:
                up, down = piece(step) + up, piece(-step) + down
        return piece(0) + up + down


def stack_kernel(*refs):
    out_ref, start = refs[-1], 0
    for ref in refs[:-1]:
        out_ref[start : start + ref.shape[0]] = ref[...]
        start += ref.shape[0]


def stack_rows(parts):
    rows = sum(part.shape[0] for part in parts)
    return pl.pallas_call(
        stack_kernel,
        out_shape=jax.ShapeDtypeStruct((rows, parts[0].shape[1]), parts[0].dtype),
        name="stack_rows",
    )(*parts)


def place_kernel(count, sources_ref, mine_ref, other_ref, out_ref):
    rows = out_ref.shape[0] // count
    for block in range(count):
        ref = mine_ref if block < count // 2 else other_ref
        start = block % (count // 2) * rows
        target = pl.multiple_of(sources_ref[block] * rows, rows)
        out_ref[pl.ds(target, rows)] = ref[start : start + rows]


def place_rows(mine, other, sources, count):
    return pl.pallas_call(
        functools.partial(place_kernel, count),
        in_specs=[
            pl.BlockSpec(memory_space=pltpu.SMEM),
            pl.BlockSpec(memory_space=pltpu.VMEM),
            pl.BlockSpec(memory_space=pltpu.VMEM),
        ],
        out_specs=pl.BlockSpec(memory_space=pltpu.VMEM),
        out_shape=jax.ShapeDtypeStruct((2 * mine.shape[0], mine.shape[1]), mine.dtype),
        name="place_rows",
    )(sources, mine, other)


def sum_over(value, axis, size):
    if size & (size - 1):
        return lax.psum(value, axis)
    distance = 1
    while distance < size:
        value = value + lax.ppermute(value, axis, [(at, at ^ distance) for at in range(size)])
        distance *= 2
    return value


def both_halves(rows, size, index):
    if size != 2:
        return lax.all_gather(rows, "tensor", axis=0, tiled=True)
    other = lax.ppermute(rows, "tensor", [(0, 1), (1, 0)])
    return jnp.where(
        index == 0, jnp.concatenate([rows, other], 0), jnp.concatenate([other, rows], 0)
    )


def sum_to_owner(product, size, index, row_count):
    if size != 2:
        whole = jnp.concatenate([product(at * row_count) for at in range(size)], 0)
        return lax.psum_scatter(
            whole.astype(BF16), "tensor", scatter_dimension=0, tiled=True
        ).astype(F32)
    sent = product((1 - index) * row_count).astype(BF16)
    got = lax.ppermute(sent, "tensor", [(0, 1), (1, 0)])
    return product(index * row_count) + got.astype(F32)


def delayed(rows, steps):
    if steps == 0:
        return rows
    at = lax.broadcasted_iota(jnp.int32, rows.shape, 0)
    return jnp.where(at >= steps, pltpu.roll(rows, steps, 0), 0.0)


def advanced(rows, steps):
    if steps == 0:
        return rows
    length = rows.shape[0]
    at = lax.broadcasted_iota(jnp.int32, rows.shape, 0)
    return jnp.where(at < length - steps, pltpu.roll(rows, length - steps, 0), 0.0)


def convolve(rows, taps, offset):
    width = taps.shape[0]
    total = offset + taps[width - 1 : width] * rows
    for tap in range(width - 1):
        total = total + taps[tap : tap + 1] * delayed(rows, width - 1 - tap)
    return total


def convolve_back(grad, rows, taps):
    width = taps.shape[0]
    total = taps[width - 1 : width] * grad
    for tap in range(width - 1):
        total = total + taps[tap : tap + 1] * advanced(grad, width - 1 - tap)
    tap_grads = [
        jnp.sum(grad * delayed(rows, width - 1 - tap), axis=0, keepdims=True)
        for tap in range(width)
    ]
    return total, tap_grads, jnp.sum(grad, axis=0, keepdims=True)


def logistic(value):
    return 1.0 / (1.0 + jnp.exp(-value))


def softplus(value):
    return jnp.maximum(value, 0.0) + jnp.log1p(jnp.exp(-jnp.abs(value)))


def head_picker(heads, head_dim, turned):
    first = pl.program_id(0) * heads
    row = lax.broadcasted_iota(jnp.int32, (LANES, LANES), 0)
    col = lax.broadcasted_iota(jnp.int32, (LANES, LANES), 1)
    if turned:
        return (col == first + row // head_dim).astype(F32)
    return (row == first + col // head_dim).astype(F32)


def exact_dot(left, right):
    return lax.dot_general(
        left, right, (((1,), (0,)), ((), ())), precision=EXACT, preferred_element_type=F32
    )


def token_state(aux_ref, bctaps_ref, bcbias_ref, headrow_ref, chunk, state, refs):
    sh_ref, turn_ref, dt_ref, cum_ref, cumt_ref = refs
    length = aux_ref.shape[0]
    width = 2 * state
    pre = convolve(aux_ref[:, :width], bctaps_ref[...], bcbias_ref[...])
    shared = pre * logistic(pre)
    sh_ref[...] = shared.astype(BF16)
    turn_ref[...] = shared.T.astype(BF16)
    timestep = softplus(aux_ref[:, width : width + LANES] + headrow_ref[0:1])
    dt_ref[...] = timestep
    decay = -jnp.exp(headrow_ref[1:2]) * timestep
    row = lax.broadcasted_iota(jnp.int32, (chunk, chunk), 0)
    col = lax.broadcasted_iota(jnp.int32, (chunk, chunk), 1)
    lower = (row >= col).astype(F32)
    for start in range(0, length, chunk):
        running = exact_dot(lower, decay[start : start + chunk])
        cum_ref[start : start + chunk] = running
        cumt_ref[:, start : start + chunk] = running.T


def mixer_kernel(
    chunk,
    head_dim,
    state,
    value_ref,
    aux_ref,
    taps_ref,
    bias_ref,
    skip_ref,
    bctaps_ref,
    bcbias_ref,
    headrow_ref,
    mixed_ref,
    states_ref,
    sh_ref,
    turn_ref,
    dt_ref,
    cum_ref,
    cumt_ref,
    prod_ref,
):
    length = value_ref.shape[0]
    heads = LANES // head_dim
    blocks = length // chunk

    @pl.when(pl.program_id(0) == 0)
    def _():
        token_state(
            aux_ref,
            bctaps_ref,
            bcbias_ref,
            headrow_ref,
            chunk,
            state,
            (sh_ref, turn_ref, dt_ref, cum_ref, cumt_ref),
        )
        for block in range(blocks):
            rows = pl.ds(block * chunk, chunk)
            prod_ref[block] = dot_last(sh_ref[rows, state:], sh_ref[rows, :state])

    pick = head_picker(heads, head_dim, False)
    pre = convolve(value_ref[...], taps_ref[...], bias_ref[...])
    values = pre * logistic(pre)
    weighted = values * exact_dot(dt_ref[...], pick)
    running = exact_dot(cum_ref[...], pick)
    lane = lax.broadcasted_iota(jnp.int32, (chunk, LANES), 1) // head_dim
    row = lax.broadcasted_iota(jnp.int32, (chunk, chunk), 0)
    col = lax.broadcasted_iota(jnp.int32, (chunk, chunk), 1)
    causal = row >= col
    held = jnp.zeros((state, LANES), F32)
    for block in range(blocks):
        start = block * chunk
        rows = slice(start, start + chunk)
        states_ref[0, block] = held
        cum = running[rows]
        wide = weighted[rows]
        out = jnp.exp(cum) * dot_mid(sh_ref[rows, state:], held.astype(BF16))
        for head in range(heads):
            number = pl.program_id(0) * heads + head
            across = cumt_ref[pl.ds(number, 1), rows]
            down = cum[:, head * head_dim : head * head_dim + 1]
            decay = jnp.exp(jnp.where(causal, down - across, -jnp.inf))
            mixing = (prod_ref[block] * decay).astype(BF16)
            out = out + dot_mid(mixing, jnp.where(lane == head, wide, 0.0).astype(BF16))
        mixed_ref[rows, :] = out + values[rows] * skip_ref[...]
        last = cum[chunk - 1 : chunk]
        ending = (wide * jnp.exp(last - cum)).astype(BF16)
        held = jnp.exp(last) * held + dot_mid(turn_ref[:state, rows], ending)


def mixer_back_kernel(
    chunk,
    head_dim,
    state,
    value_ref,
    aux_ref,
    grad_ref,
    states_ref,
    taps_ref,
    bias_ref,
    skip_ref,
    bctaps_ref,
    bcbias_ref,
    headrow_ref,
    value_grad_ref,
    lane_ref,
    shared_grad_ref,
    step_grad_ref,
    head_grad_ref,
    sh_ref,
    turn_ref,
    dt_ref,
    cum_ref,
    cumt_ref,
    prod_ref,
    prod_grad_ref,
    b_grad_ref,
    c_grad_ref,
    dcum_ref,
    dcumt_ref,
    ddt_ref,
    conv_grad_ref,
):
    length = value_ref.shape[0]
    heads = LANES // head_dim
    blocks = length // chunk
    width = taps_ref.shape[0]

    @pl.when(pl.program_id(0) == 0)
    def _():
        token_state(
            aux_ref,
            bctaps_ref,
            bcbias_ref,
            headrow_ref,
            chunk,
            state,
            (sh_ref, turn_ref, dt_ref, cum_ref, cumt_ref),
        )
        for block in range(blocks):
            rows = pl.ds(block * chunk, chunk)
            prod_ref[block] = dot_last(sh_ref[rows, :state], sh_ref[rows, state:])
        for ref in (prod_grad_ref, b_grad_ref, c_grad_ref, dcum_ref, dcumt_ref, ddt_ref):
            ref[...] = jnp.zeros(ref.shape, ref.dtype)

    pick = head_picker(heads, head_dim, False)
    collect = head_picker(heads, head_dim, True)
    pre = convolve(value_ref[...], taps_ref[...], bias_ref[...])
    sig = logistic(pre)
    values = pre * sig
    slope = sig * (1.0 + pre * (1.0 - sig))
    timestep = exact_dot(dt_ref[...], pick)
    running = exact_dot(cum_ref[...], pick)
    weighted = values * timestep
    lane = lax.broadcasted_iota(jnp.int32, (chunk, LANES), 1) // head_dim
    lane_at = lax.broadcasted_iota(jnp.int32, (chunk, LANES), 1)
    row_at = lax.broadcasted_iota(jnp.int32, (chunk, LANES), 0)
    row = lax.broadcasted_iota(jnp.int32, (chunk, chunk), 0)
    col = lax.broadcasted_iota(jnp.int32, (chunk, chunk), 1)
    causal = row <= col
    leaving = jnp.zeros((state, LANES), F32)
    for block in reversed(range(blocks)):
        start = block * chunk
        rows = slice(start, start + chunk)
        cum = running[rows]
        wide = weighted[rows]
        grad = grad_ref[rows, :]
        held = states_ref[0, block]
        held_b = held.astype(BF16)
        leaving_b = leaving.astype(BF16)
        last = cum[chunk - 1 : chunk]
        since = jnp.exp(cum)
        until = jnp.exp(last - cum)
        decayed = jnp.exp(last)
        ending = wide * until
        from_state = dot_mid(sh_ref[rows, :state], leaving_b)
        wide_grad = until * from_state
        b_grad_ref[rows, :] += dot_last(ending.astype(BF16), leaving_b)
        carried = dot_mid(sh_ref[rows, state:], held_b)
        begun = grad * since
        begun_b = begun.astype(BF16)
        c_grad_ref[rows, :] += dot_last(begun_b, held_b)
        into = ending * from_state
        at_end = jnp.sum(into, axis=0, keepdims=True) + decayed * jnp.sum(
            leaving * held, axis=0, keepdims=True
        )
        cum_part = begun * carried - into + jnp.where(row_at == chunk - 1, at_end, 0.0)
        dcum = dcum_ref[rows, :] + exact_dot(cum_part, collect)
        for head in range(heads):
            number = pl.program_id(0) * heads + head
            across = cumt_ref[pl.ds(number, 1), rows]
            down = cum[:, head * head_dim : head * head_dim + 1]
            decay = jnp.exp(jnp.where(causal, across - down, -jnp.inf))
            grad_head = jnp.where(lane == head, grad, 0.0).astype(BF16)
            wide_head = jnp.where(lane == head, wide, 0.0).astype(BF16)
            product = prod_ref[block]
            mixing = (product * decay).astype(BF16)
            wide_grad = wide_grad + dot_mid(mixing, grad_head)
            scored = dot_last(wide_head, grad_head) * decay
            prod_grad_ref[block] += scored
            pairs = scored * product
            dcumt_ref[pl.ds(number, 1), rows] = jnp.sum(pairs, axis=0, keepdims=True)
            sent = jnp.sum(pairs, axis=1, keepdims=True)
            dcum = dcum - jnp.where(lane_at == number, sent, 0.0)
        dcum_ref[rows, :] = dcum
        ddt_ref[rows, :] += exact_dot(wide_grad * values[rows], collect)
        conv_grad_ref[rows, :] = (wide_grad * timestep[rows] + grad * skip_ref[...]) * slope[rows]
        leaving = decayed * leaving + dot_mid(turn_ref[state:, rows], begun_b)
    value_grad, tap_grads, bias_grad = convolve_back(
        conv_grad_ref[...], value_ref[...], taps_ref[...]
    )
    value_grad_ref[...] = value_grad.astype(BF16)
    skip_grad = jnp.sum(grad_ref[...] * values, axis=0, keepdims=True)
    for tap in range(width):
        lane_ref[tap : tap + 1] = tap_grads[tap]
    lane_ref[width : width + 1] = bias_grad
    lane_ref[width + 1 : width + 2] = skip_grad

    @pl.when(pl.program_id(0) == pl.num_programs(0) - 1)
    def _():
        rate = -jnp.exp(headrow_ref[1:2])
        upper = (row <= col).astype(F32)
        shift_sum = jnp.zeros((1, LANES), F32)
        rate_sum = jnp.zeros((1, LANES), F32)
        for block in range(blocks):
            start = block * chunk
            rows = slice(start, start + chunk)
            scored = prod_grad_ref[block].astype(BF16)
            shared_grad_ref[rows, :state] = (
                b_grad_ref[rows, :] + dot_mid(scored, sh_ref[rows, state:])
            ).astype(shared_grad_ref.dtype)
            shared_grad_ref[rows, state:] = (
                c_grad_ref[rows, :] + dot_first(scored, sh_ref[rows, :state])
            ).astype(shared_grad_ref.dtype)
            decay_grad = exact_dot(upper, dcum_ref[rows, :] + dcumt_ref[:, rows].T)
            rate_sum = rate_sum + jnp.sum(
                decay_grad * rate * dt_ref[rows, :], axis=0, keepdims=True
            )
            step = aux_ref[rows, 2 * state : 2 * state + LANES] + headrow_ref[0:1]
            step_grad = (ddt_ref[rows, :] + decay_grad * rate) * logistic(step)
            shift_sum = shift_sum + jnp.sum(step_grad, axis=0, keepdims=True)
            step_grad_ref[rows, :] = step_grad.astype(BF16)
        head_grad_ref[0:1] = shift_sum
        head_grad_ref[1:2] = rate_sum


def bc_back_kernel(state, sums, aux_ref, mine_ref, other_ref, taps_ref, bias_ref, grad_ref, small_ref):
    width = taps_ref.shape[0]
    rows = aux_ref[:, : 2 * state]
    pre = convolve(rows, taps_ref[...], bias_ref[...])
    sig = logistic(pre)
    total = mine_ref[...].astype(F32)
    if sums:
        total = total + other_ref[...].astype(F32)
    grad, tap_grads, bias_grad = convolve_back(
        total * (sig * (1.0 + pre * (1.0 - sig))), rows, taps_ref[...]
    )
    grad_ref[...] = grad.astype(BF16)
    for tap in range(width):
        small_ref[tap : tap + 1] = tap_grads[tap]
    small_ref[width : width + 1] = bias_grad


def chunk_of(length):
    for chunk in (256, 128):
        if length % chunk == 0:
            return chunk
    return length


def whole(shape):
    return pl.BlockSpec(shape, lambda at: (0,) * len(shape))


def lanes_of(rows):
    return pl.BlockSpec((rows, LANES), lambda at: (0, at))


def shared_scratch(length, chunk, state):
    return [
        pltpu.VMEM((length, 2 * state), BF16),
        pltpu.VMEM((2 * state, length), BF16),
        pltpu.VMEM((length, LANES), F32),
        pltpu.VMEM((length, LANES), F32),
        pltpu.VMEM((LANES, length), F32),
        pltpu.VMEM((length // chunk, chunk, chunk), F32),
    ]


def mixer(value_pre, aux_pre, taps, bias, skip, bc_taps, bc_bias, head_rows, head_dim):
    length, inner = value_pre.shape
    state = bc_taps.shape[1] // 2
    chunk = chunk_of(length)
    blocks = length // chunk
    programs = inner // LANES
    return pl.pallas_call(
        functools.partial(mixer_kernel, chunk, head_dim, state),
        grid=(programs,),
        in_specs=[
            lanes_of(length),
            whole(aux_pre.shape),
            lanes_of(taps.shape[0]),
            lanes_of(1),
            lanes_of(1),
            whole(bc_taps.shape),
            whole(bc_bias.shape),
            whole(head_rows.shape),
        ],
        out_specs=[
            lanes_of(length),
            pl.BlockSpec((1, blocks, state, LANES), lambda at: (at, 0, 0, 0)),
        ],
        out_shape=[
            jax.ShapeDtypeStruct((length, inner), F32),
            jax.ShapeDtypeStruct((programs, blocks, state, LANES), F32),
        ],
        scratch_shapes=shared_scratch(length, chunk, state),
        name="mixer",
        cost_estimate=pl.CostEstimate(
            flops=4 * length * chunk * inner, bytes_accessed=8 * length * inner, transcendentals=0
        ),
    )(value_pre, aux_pre, taps, bias, skip, bc_taps, bc_bias, head_rows)


def mixer_back(
    value_pre, aux_pre, mixed_grad, states, taps, bias, skip, bc_taps, bc_bias, head_rows, head_dim
):
    length, inner = value_pre.shape
    state = bc_taps.shape[1] // 2
    chunk = chunk_of(length)
    blocks = length // chunk
    programs = inner // LANES
    lane_rows = 8 * ((taps.shape[0] + 2 + 7) // 8)
    return pl.pallas_call(
        functools.partial(mixer_back_kernel, chunk, head_dim, state),
        grid=(programs,),
        in_specs=[
            lanes_of(length),
            whole(aux_pre.shape),
            lanes_of(length),
            pl.BlockSpec((1, blocks, state, LANES), lambda at: (at, 0, 0, 0)),
            lanes_of(taps.shape[0]),
            lanes_of(1),
            lanes_of(1),
            whole(bc_taps.shape),
            whole(bc_bias.shape),
            whole(head_rows.shape),
        ],
        out_specs=[
            lanes_of(length),
            lanes_of(lane_rows),
            whole((length, 2 * state)),
            whole((length, LANES)),
            whole((8, LANES)),
        ],
        out_shape=[
            jax.ShapeDtypeStruct((length, inner), BF16),
            jax.ShapeDtypeStruct((lane_rows, inner), F32),
            jax.ShapeDtypeStruct((length, 2 * state), F32),
            jax.ShapeDtypeStruct((length, LANES), BF16),
            jax.ShapeDtypeStruct((8, LANES), F32),
        ],
        scratch_shapes=shared_scratch(length, chunk, state)
        + [
            pltpu.VMEM((blocks, chunk, chunk), F32),
            pltpu.VMEM((length, state), F32),
            pltpu.VMEM((length, state), F32),
            pltpu.VMEM((length, LANES), F32),
            pltpu.VMEM((LANES, length), F32),
            pltpu.VMEM((length, LANES), F32),
            pltpu.VMEM((length, LANES), F32),
        ],
        name="mixer_back",
        cost_estimate=pl.CostEstimate(
            flops=12 * length * chunk * inner, bytes_accessed=16 * length * inner, transcendentals=0
        ),
    )(value_pre, aux_pre, mixed_grad, states, taps, bias, skip, bc_taps, bc_bias, head_rows)


def bc_back(aux_pre, mine, other, taps, bias):
    length = aux_pre.shape[0]
    state = taps.shape[1] // 2
    rows = 8 * ((taps.shape[0] + 1 + 7) // 8)
    return pl.pallas_call(
        functools.partial(bc_back_kernel, state, other is not None),
        out_shape=[
            jax.ShapeDtypeStruct((length, 2 * state), BF16),
            jax.ShapeDtypeStruct((rows, 2 * state), F32),
        ],
        name="bc_back",
    )(aux_pre, mine, mine if other is None else other, taps, bias)


def per_device(
    layer_input,
    norm_gain,
    gate_proj,
    value_proj,
    bc_proj,
    step_proj,
    out_proj,
    value_taps,
    value_bias,
    bc_taps,
    bc_bias,
    step_shift,
    log_rate,
    skip_gain,
    gate_gain,
    cotangent,
):
    tensor_size = lax.axis_size("tensor")
    dp_size = lax.axis_size("dp")
    index = lax.axis_index("tensor")
    row_count, features = layer_input.shape
    heads = step_shift.shape[0]
    inner = gate_proj.shape[1]
    head_dim = inner // heads
    inner_width = inner * tensor_size
    bc_width = bc_proj.shape[1]
    taps_width = value_taps.shape[0]
    ring = Ring(dp_size)
    shard = features // dp_size
    half = features // 2
    rows_of = functools.partial(lax.dynamic_slice_in_dim, slice_size=row_count, axis=0)

    aux_width = bc_width + LANES
    filler = jnp.zeros((shard, LANES - heads - 1), BF16)
    first_shard = jnp.concatenate(
        [value_proj, bc_proj, step_proj, norm_gain[:, None], filler], axis=1
    )
    sources = ring.sources()
    first_w = ring.gather(first_shard, sources)
    later_w = ring.gather(jnp.concatenate([gate_proj, out_proj.T], axis=1), sources)
    x_all = both_halves(layer_input, tensor_size, index)
    cot_all = both_halves(cotangent, tensor_size, index)
    value_w, bc_w = first_w[:, :inner], first_w[:, inner : inner + bc_width]
    step_w = first_w[:, inner + bc_width :]
    gate_w, out_w = later_w[:, :inner], later_w[:, inner:]
    gain = first_w[:, inner + bc_width + heads].astype(F32)[None, :]

    x_f32 = x_all.astype(F32)
    inverse = lax.rsqrt(jnp.mean(x_f32 * x_f32, axis=-1, keepdims=True) + EPS)
    normed = (x_f32 * inverse * gain).astype(BF16)
    value_pre = dot_mid(normed, value_w)
    aux_pre = dot_mid(normed, first_w[:, inner:])

    at = (sources[:, None] * shard + jnp.arange(shard)[None, :]).reshape(1, features)
    reorder = (jnp.arange(features)[:, None] == at).astype(BF16)
    normed_turned = dot_mid(normed, reorder, BF16)
    cot_turned = dot_mid(cot_all, reorder, BF16)

    def weight_grads(left, right):
        return dot_first(left[:, :half], right), dot_first(left[:, half:], right, BF16)

    skip = jnp.repeat(skip_gain, head_dim)[None, :]
    head_rows = jnp.zeros((8, LANES), F32)
    head_rows = head_rows.at[0, :heads].set(step_shift).at[1, :heads].set(log_rate)
    bias = value_bias[None, :]
    bc_offset = bc_bias[None, :]
    mixed, states = mixer(
        value_pre, aux_pre, value_taps, bias, skip, bc_taps, bc_offset, head_rows, head_dim
    )
    gate_pre = dot_mid(normed, gate_w)
    normed_out = dot_mid(cot_all, out_w)
    sigmoid = jax.nn.sigmoid(gate_pre)
    gate_act = gate_pre * sigmoid
    gated = mixed * gate_act
    scaled = normed_out * gate_gain[None, :]
    stats = sum_over(
        jnp.stack([jnp.sum(gated * gated, axis=1), jnp.sum(scaled * gated, axis=1)]),
        "tensor",
        tensor_size,
    )
    inv_rms = lax.rsqrt(stats[0] / inner_width + EPS)[:, None]
    gated_norm = (gated * inv_rms * gate_gain[None, :]).astype(BF16)
    gating_part = jnp.sum(normed_out * gated * inv_rms, axis=0)
    gated_grad = inv_rms * scaled - gated * inv_rms * inv_rms * inv_rms * (
        stats[1] / inner_width
    )[:, None]
    mixed_grad = gated_grad * gate_act
    gate_round = (
        gated_grad * mixed * sigmoid * (1.0 + gate_pre * (1.0 - sigmoid))
    ).astype(BF16)
    out_parts = weight_grads(cot_turned, gated_norm)
    gate_parts = weight_grads(normed_turned, gate_round)
    early = ring.scatter_sum(
        *(jnp.concatenate(both, axis=1) for both in zip(gate_parts, out_parts))
    )
    gate_grad, out_grad = early[:, :inner], early[:, inner:]
    out_sum = sum_to_owner(
        lambda start: dot_last(rows_of(gated_norm, start), out_w),
        tensor_size,
        index,
        row_count,
    )
    rows_f32 = layer_input.astype(F32)
    layer_output = (out_sum + rows_f32).astype(BF16)

    value_round, lane_grads, shared_grad, step_round, head_grads = mixer_back(
        value_pre,
        aux_pre,
        mixed_grad,
        states,
        value_taps,
        bias,
        skip,
        bc_taps,
        bc_offset,
        head_rows,
        head_dim,
    )
    if tensor_size == 2:
        shared_sent = shared_grad.astype(BF16)
        shared_other = lax.ppermute(shared_sent, "tensor", [(0, 1), (1, 0)])
    else:
        shared_sent, shared_other = lax.psum(shared_grad, "tensor"), None
    bc_round, bc_small = bc_back(aux_pre, shared_sent, shared_other, bc_taps, bc_offset)
    value_grad = ring.scatter_sum(*weight_grads(normed_turned, value_round))
    aux_round = jnp.concatenate([bc_round, step_round], axis=1)
    aux_part = dot_first(normed, aux_round, BF16).reshape(dp_size, shard, aux_width)
    aux_grad = jnp.sum(lax.all_to_all(aux_part, "dp", 0, 0).astype(F32), axis=0)
    bc_grad = aux_grad[:, :bc_width]
    step_grad = aux_grad[:, bc_width : bc_width + heads]

    def feature_grads(start):
        return (
            dot_last(rows_of(gate_round, start), gate_w)
            + dot_last(rows_of(value_round, start), value_w)
            + dot_last(rows_of(step_round, start), step_w)
        )

    input_part = sum_to_owner(feature_grads, tensor_size, index, row_count)
    input_part = input_part + dot_last(rows_of(bc_round, index * row_count), bc_w)

    own_inverse = lax.rsqrt(jnp.mean(rows_f32 * rows_f32, axis=-1, keepdims=True) + EPS)
    gained = input_part * gain
    across = jnp.sum(gained * rows_f32, axis=-1, keepdims=True) / features
    input_grad = (
        own_inverse * gained
        - rows_f32 * own_inverse * own_inverse * own_inverse * across
        + cotangent.astype(F32)
    )
    gained_sum = jnp.sum(
        gate_proj.astype(F32) * gate_grad + value_proj.astype(F32) * value_grad, axis=1
    )
    gained_sum = gained_sum + jnp.sum(step_proj.astype(F32) * step_grad, axis=1)
    gained_sum = gained_sum + jnp.sum(bc_proj.astype(F32) * bc_grad, axis=1) / tensor_size
    gain_grad = sum_over(gained_sum, "tensor", tensor_size) / norm_gain.astype(F32)

    lane_sums = jnp.concatenate(
        [lane_grads[: taps_width + 2], gating_part[None, :]], axis=0
    ).reshape(-1, LANES)
    bc_sums = bc_small[: taps_width + 1].reshape(-1, LANES)
    sums = sum_over(
        jnp.concatenate([lane_sums, bc_sums, head_grads[:2]], axis=0), "dp", dp_size
    )
    lane_count, bc_count = lane_sums.shape[0], bc_sums.shape[0]
    lane_total = sums[:lane_count].reshape(taps_width + 3, inner)
    bc_total = sums[lane_count : lane_count + bc_count].reshape(taps_width + 1, bc_width)
    head_total = sums[lane_count + bc_count :]
    return (
        layer_output,
        input_grad,
        gain_grad,
        gate_grad,
        value_grad,
        bc_grad,
        step_grad,
        out_grad.T,
        lane_total[:taps_width],
        lane_total[taps_width],
        bc_total[:taps_width],
        bc_total[taps_width],
        head_total[0, :heads],
        head_total[1, :heads],
        jnp.sum(lane_total[taps_width + 1].reshape(heads, head_dim), axis=1),
        lane_total[taps_width + 2],
    )


def solution(mesh):
    in_specs = (
        P(("dp", "tensor"), None),
        P("dp"),
        P("dp", "tensor"),
        P("dp", "tensor"),
        P("dp", None),
        P("dp", "tensor"),
        P("tensor", "dp"),
        P(None, "tensor"),
        P("tensor"),
        P(),
        P(),
        P("tensor"),
        P("tensor"),
        P("tensor"),
        P("tensor"),
        P(("dp", "tensor"), None),
    )
    out_specs = (
        P(("dp", "tensor"), None),
        P(("dp", "tensor"), None),
        P("dp"),
        P("dp", "tensor"),
        P("dp", "tensor"),
        P("dp", None),
        P("dp", "tensor"),
        P("tensor", "dp"),
        P(None, "tensor"),
        P("tensor"),
        P(),
        P(),
        P("tensor"),
        P("tensor"),
        P("tensor"),
        P("tensor"),
    )
    return jax.shard_map(
        per_device, mesh=mesh, in_specs=in_specs, out_specs=out_specs, check_vma=False
    )
```
